32 devices in a mesh: dp: 8 (over y, x, core), seq: 4 (over z).
Axes of the slice: x: 2, y: 2, z: 4, core: 2. Of those that a mesh axis runs over, the one named last changes fastest.
Arguments:
- tokens: bfloat16 [32, 1024, 768], P('dp', 'seq'), may hold values from -6 to 6
- cotangent: bfloat16 [32, 1024, 768], P('dp', 'seq'), may hold values from -6 to 6
- segments: int32 [32, 1024], P('dp'), may hold values from 0 to 4, as said below
- keep_flags: int32 [32, 8], P('dp'), may hold values 0 or 1
- first_gain: float32 [768], P('dp'), may hold values from 0.5 to 1.5
- first_shift: float32 [768], P('dp'), may hold values from -1.2 to 1.2
- joint_weight: float32 [768, 2304], P('dp'), may hold values from -0.21875 to 0.21875
- joint_bias: float32 [1536], P('dp'), may hold values from -1.2 to 1.2
- output_weight: float32 [768, 768], P('dp'), may hold values from -3 to 3
- output_bias: float32 [768], P('dp'), may hold values from -1.2 to 1.2
- second_gain: float32 [768], P('dp'), may hold values from 0.5 to 1.5
- second_shift: float32 [768], P('dp'), may hold values from -1.2 to 1.2
- expand_weight: float32 [768, 3072], P('dp'), may hold values from -0.21875 to 0.21875
- expand_bias: float32 [3072], P('dp'), may hold values from -1.2 to 1.2
- reduce_weight: float32 [3072, 768], P('dp'), may hold values from -0.109375 to 0.109375
- reduce_bias: float32 [768], P('dp'), may hold values from -1.2 to 1.2
Outputs:
- output: bfloat16 [32, 1024, 768], P('dp', 'seq')
- grad_tokens: float32 [32, 1024, 768], P('dp', 'seq')
- first_gain_grad: float32 [768], P('dp')
- first_shift_grad: float32 [768], P('dp')
- joint_weight_grad: float32 [768, 2304], P('dp')
- joint_bias_grad: float32 [1536], P('dp')
- output_weight_grad: float32 [768, 768], P('dp')
- output_bias_grad: float32 [768], P('dp')
- second_gain_grad: float32 [768], P('dp')
- second_shift_grad: float32 [768], P('dp')
- expand_weight_grad: float32 [768, 3072], P('dp')
- expand_bias_grad: float32 [3072], P('dp')
- reduce_weight_grad: float32 [3072, 768], P('dp')
- reduce_bias_grad: float32 [768], P('dp')
The draws below stay inside these ranges and needn't reach their ends.
Inputs may be any that keep to these rules, and one draw needn't show every extreme that they name: `segments`: positions 0 to 7 of each row hold image p // 2 (class token at even p, distillation token at odd p); then the patch tokens of images 0 to 3 follow in this order, each image's patches contiguous and one or more; the rest of the row, never empty, is padding with the value 4. `keep_flags`: column i < 4 keeps the attention branch of image i, column 4 + i its feed-forward branch.
All inputs are finite; a program needn't handle non-finite values. No bound on the sum of `keep_flags` on one device may be relied on, other than what follows from the above.
Results may differ from the reference program's by a relative error of at most 0.012.
The reference program's roundings to bfloat16 on the way count: a program that leaves them out, or rounds other values in their place, can miss the bound.
Values may be sent and summed in bfloat16 or wider, within the bound.
No kernel may reach another device: no remote copies, remote signals or barrier semaphores. Data moves between devices by JAX's collectives and lax.ppermute only.
A program may use at most 192 MiB of HBM per device.

```python
import math
import jax
import jax.numpy as jnp
from jax import lax

D = 768
HEADS = 12
HEAD = 64
FF = 3072
ROW_LEN = 1024
IMGS = 4
ROWS = 32


def draw_segments(key, part):
    capacity = ROW_LEN - 2 * IMGS
    patch_counts = jax.random.randint(key, (ROWS, IMGS), capacity // 8, capacity // 4)
    ends_at = jnp.cumsum(patch_counts, axis=1)
    places = jnp.arange(ROW_LEN, dtype=jnp.int32)
    offset_in = places - 2 * IMGS
    patch_ids = jnp.sum((offset_in[None, :, None] >= ends_at[:, None, :]).astype(jnp.int32), axis=-1)
    special = jnp.broadcast_to(places // 2, (ROWS, ROW_LEN))
    return jnp.where(places[None, :] < 2 * IMGS, special, patch_ids).astype(jnp.int32)


def touch_ends(drawn, stream_key, low, largest):
    shape = drawn.shape
    spot = [jax.random.randint(jax.random.fold_in(stream_key, axis), (), 0, shape[axis]) for axis in range(len(shape))]
    drawn = drawn.at[tuple(spot)].set(low)
    longest = shape.index(max(shape))
    spot[longest] = (spot[longest] + 1) % shape[longest]
    return drawn.at[tuple(spot)].set(largest)


def levels(stream_key, shape, pieces, smallest, high):
    level = 1.0
    for position, blocks in pieces:
        steps = jax.random.uniform(jax.random.fold_in(jax.random.fold_in(stream_key, 6), position), (blocks,), jnp.float32, smallest / len(pieces), high / len(pieces))
        level = level * jnp.repeat(jnp.exp(steps), shape[position] // blocks).reshape((-1,) + (1,) * (len(shape) - 1 - position))
    return level


def noise(stream_key, dims, scale, bound, cuts=(), kind=jnp.bfloat16):
    loudness = levels(stream_key, dims, cuts, -0.22, 0.18) if cuts else 1.0
    entries = jax.random.normal(stream_key, dims, jnp.float32) * scale * loudness
    return jnp.minimum(jnp.maximum(entries, -bound), bound).astype(kind)


def setup_inputs(seed: int = 0) -> dict:
    streams_of = jax.random.split(jax.random.key(seed), 17)
    tokens = noise(streams_of[0], (ROWS, ROW_LEN, D), 1.0, 6.0, ((0, 8), (1, 4)))
    cotangent = noise(streams_of[1], (ROWS, ROW_LEN, D), 1.0, 6.0, ((0, 8), (1, 4)))
    segments = draw_segments(jax.random.fold_in(streams_of[16], 71), 0)
    keep_flags = touch_ends((jax.random.randint(streams_of[3], (ROWS, 2 * IMGS), 0, 10) < 9).astype(jnp.int32), jax.random.fold_in(streams_of[3], 1), 0, 1)
    first_gain = jnp.clip(1.0 + 0.1 * jax.random.normal(streams_of[4], (D,), jnp.float32), 0.5, 1.5)
    first_shift = noise(streams_of[5], (D,), 0.2, 1.2, ((0, 8),), jnp.float32)
    joint_weight = noise(streams_of[6], (D, 3 * D), D ** -0.5, 0.21875, ((0, 8),), jnp.float32)
    joint_bias = noise(streams_of[7], (2 * D,), 0.2, 1.2, ((0, 8),), jnp.float32)
    output_weight = noise(streams_of[8], (D, D), 4 ** -0.5, 3.0, ((0, 8),), jnp.float32)
    output_bias = noise(streams_of[9], (D,), 0.2, 1.2, ((0, 8),), jnp.float32)
    second_gain = jnp.clip(1.0 + 0.1 * jax.random.normal(streams_of[10], (D,), jnp.float32), 0.5, 1.5)
    second_shift = noise(streams_of[11], (D,), 0.2, 1.2, ((0, 8),), jnp.float32)
    expand_weight = noise(streams_of[12], (D, FF), D ** -0.5, 0.21875, ((0, 8),), jnp.float32)
    expand_bias = noise(streams_of[13], (FF,), 0.2, 1.2, ((0, 8),), jnp.float32)
    reduce_weight = noise(streams_of[14], (FF, D), FF ** -0.5, 0.109375, ((0, 8),), jnp.float32)
    reduce_bias = noise(streams_of[15], (D,), 0.2, 1.2, ((0, 8),), jnp.float32)
    return dict(tokens=tokens, cotangent=cotangent, segments=segments, keep_flags=keep_flags, first_gain=first_gain, first_shift=first_shift, joint_weight=joint_weight, joint_bias=joint_bias, output_weight=output_weight, output_bias=output_bias, second_gain=second_gain, second_shift=second_shift, expand_weight=expand_weight, expand_bias=expand_bias, reduce_weight=reduce_weight, reduce_bias=reduce_bias)


keep_ratio_inverse = 1.0 / 0.9
score_factor = 0.125
norm_epsilon = 1e-06

@jax.custom_vjp
def low(v):
    return lax.optimization_barrier(v.astype(jnp.bfloat16)).astype(jnp.float32)

@jax.custom_vjp
def low_back(v):
    return v

def low_keep(v):
    return (low(v), None)

def low_pass(kept, grad):
    return (grad,)

def back_keep(v):
    return (v, None)

def back_low(kept, grad):
    return (low(grad),)
low.defvjp(low_keep, low_pass)
low_back.defvjp(back_keep, back_low)

def layer_norm(inputs, gain, shift_b):
    centre = inputs - lax.optimization_barrier(jnp.mean(inputs, axis=-1, keepdims=True))
    spread = lax.optimization_barrier(jnp.mean(centre * centre, axis=-1, keepdims=True))
    return centre * lax.rsqrt(spread + norm_epsilon) * gain + shift_b

def product(left, right):
    return jnp.dot(left, right, precision=lax.Precision.HIGHEST)

def attend_row(row_data):
    queries, key_rows, value_rows, seg_row = row_data
    raw_scores = jnp.einsum('shd,lhd->hsl', queries, key_rows, precision=lax.Precision.HIGHEST) * score_factor
    raw_scores = low_back(raw_scores)
    allowed = seg_row[:, None] == seg_row[None, :]
    masked = jnp.where(allowed[None, :, :], raw_scores, -1e+30)
    attention = low(jax.nn.softmax(masked, axis=-1))
    mixed_rows = jnp.einsum('hsl,lhd->shd', attention, value_rows, precision=lax.Precision.HIGHEST)
    return low(low_back(mixed_rows))

def group_forward(params, inputs, seg_group, scale_a, scale_b):
    gain_a, shift_a, weight_qkv, bias_qv, weight_out, bias_out, gain_b, shift_bb, weight_up, bias_up, weight_down, bias_down = tuple((low(member) for member in params))
    groups, row_len, features = inputs.shape
    flat_in = inputs.reshape(groups * row_len, features)
    normed_a = low(layer_norm(flat_in, gain_a, shift_a))
    bias_full = jnp.concatenate([bias_qv[:features], jnp.zeros((features,), bias_qv.dtype), bias_qv[features:]])
    projected = low(low_back(product(normed_a, weight_qkv) + bias_full))
    heads_shape = (groups, row_len, HEADS, HEAD)
    queries = projected[:, :features].reshape(heads_shape)
    key_rows = projected[:, features:2 * features].reshape(heads_shape)
    value_rows = projected[:, 2 * features:].reshape(heads_shape)
    mixed_rows = lax.map(jax.checkpoint(attend_row), (queries, key_rows, value_rows, seg_group))
    mixed_rows = mixed_rows.reshape(groups * row_len, features)
    branch_a = low_back(product(mixed_rows, weight_out) + bias_out)
    middle = flat_in + scale_a.reshape(-1, 1) * branch_a
    normed_b = low(layer_norm(middle, gain_b, shift_bb))
    pre_act = low_back(product(normed_b, weight_up) + bias_up)
    activated = low(jax.nn.gelu(pre_act, approximate=False))
    branch_b = low_back(product(activated, weight_down) + bias_down)
    return (middle + scale_b.reshape(-1, 1) * branch_b).reshape(groups, row_len, features)

def reference(tokens, cotangent, segments, keep_flags, first_gain, first_shift, joint_weight, joint_bias, output_weight, output_bias, second_gain, second_shift, expand_weight, expand_bias, reduce_weight, reduce_bias):
    row_count, row_len, features = tokens.shape
    images = keep_flags.shape[1] // 2
    labels = jnp.arange(images, dtype=jnp.int32)
    onehot = (segments[:, :, None] == labels[None, None, :]).astype(jnp.float32)
    flags = keep_flags.astype(jnp.float32)
    attn_scale = lax.optimization_barrier(jnp.sum(onehot * flags[:, None, :images], axis=-1)) * keep_ratio_inverse
    mlp_scale = lax.optimization_barrier(jnp.sum(onehot * flags[:, None, images:], axis=-1)) * keep_ratio_inverse
    masters = (first_gain, first_shift, joint_weight, joint_bias, output_weight, output_bias, second_gain, second_shift, expand_weight, expand_bias, reduce_weight, reduce_bias)
    group_size = math.gcd(row_count, 4)
    blocks = row_count // group_size

    def split(member):
        return member.reshape((blocks, group_size) + member.shape[1:])

    def group_step(totals, group_data):
        x_group, cot_group, seg_group, scale_a, scale_b = group_data

        def closed(params, inputs):
            return group_forward(params, inputs, seg_group, scale_a, scale_b)
        result, pullback = jax.vjp(closed, masters, x_group)
        grad_params, grad_inputs = pullback(cot_group)
        summed = tuple((running + fresh for running, fresh in zip(totals, grad_params)))
        return (summed, (result, grad_inputs))
    initial = tuple((jnp.zeros_like(member) for member in masters))
    finals, (results, grad_in) = lax.scan(group_step, initial, (split(tokens.astype(jnp.float32)), split(cotangent.astype(jnp.float32)), split(segments), split(attn_scale), split(mlp_scale)))
    output = results.reshape(tokens.shape).astype(jnp.bfloat16)
    grad_tokens = grad_in.reshape(tokens.shape)
    g_first_gain, g_first_shift, g_joint_weight, g_joint_bias, g_output_weight, g_output_bias, g_second_gain, g_second_shift, g_expand_weight, g_expand_bias, g_reduce_weight, g_reduce_bias = finals
    return (output, grad_tokens, g_first_gain, g_first_shift, g_joint_weight, g_joint_bias, g_output_weight, g_output_bias, g_second_gain, g_second_shift, g_expand_weight, g_expand_bias, g_reduce_weight, g_reduce_bias)
```

```python
import functools

import jax
import jax.numpy as jnp
from jax import lax
from jax.experimental import pallas as pl
from jax.experimental.pallas import tpu as pltpu
from jax.sharding import PartitionSpec as P

HEAD = 64
PAIR = 2 * HEAD
VIRTUAL = 8
keep_ratio_inverse = 1.0 / 0.9
norm_epsilon = 1e-06
F32 = jnp.float32
BF16 = jnp.bfloat16


def dot_nn(left, right):
    return lax.dot_general(left, right, (((1,), (0,)), ((), ())), preferred_element_type=F32)


def dot_nt(left, right):
    return lax.dot_general(left, right, (((1,), (1,)), ((), ())), preferred_element_type=F32)


def dot_tn(left, right):
    return lax.dot_general(left, right, (((0,), (0,)), ((), ())), preferred_element_type=F32)


def whole(shape):
    return pl.BlockSpec(shape, lambda *_: (0,) * len(shape))


SMEM = pl.BlockSpec(memory_space=pltpu.SMEM)
ANY = pl.BlockSpec(memory_space=pl.ANY)


def branch_scale(segment_column, flags_ref, first, images):
    scale = jnp.zeros(segment_column.shape, F32)
    for image in range(images):
        flag = flags_ref[first + image].astype(F32) * keep_ratio_inverse
        scale = jnp.where(segment_column == image, flag, scale)
    return scale


def norm_parts(inputs):
    centre = inputs - jnp.mean(inputs, axis=-1, keepdims=True)
    spread = jnp.mean(centre * centre, axis=-1, keepdims=True)
    inverse = lax.rsqrt(spread + norm_epsilon)
    return centre * inverse, inverse


def norm_backward(normal, inverse, grads, gain):
    scaled = grads * gain
    mean_scaled = jnp.mean(scaled, axis=-1, keepdims=True)
    mean_product = jnp.mean(scaled * normal, axis=-1, keepdims=True)
    return (scaled - mean_scaled - normal * mean_product) * inverse


def accumulate(step, ref, value):
    @pl.when(step == 0)
    def _():
        ref[...] = value

    @pl.when(step > 0)
    def _():
        ref[...] += value


def joint_kernel(rows, place_ref, x_ref, gain_ref, shift_ref, bias_ref, *refs):
    pieces = refs[:VIRTUAL]
    proj_ref, normed_t_ref, weight_ref, sems = refs[VIRTUAL:]

    @pl.when(pl.program_id(0) == 0)
    def _():
        copies = []
        for k in range(VIRTUAL):
            start = pl.multiple_of((place_ref[0] ^ k) * rows, 16)
            copies.append(
                pltpu.make_async_copy(
                    pieces[k].at[pl.ds(0, rows)], weight_ref.at[pl.ds(start, rows)], sems.at[k]
                )
            )
        for copy in copies:
            copy.start()
        for copy in copies:
            copy.wait()

    normal, _ = norm_parts(x_ref[...].astype(F32))
    normed = (normal * gain_ref[...] + shift_ref[...]).astype(BF16)
    normed_t_ref[...] = normed.T
    proj_ref[...] = (dot_nn(normed, weight_ref[...]) + bias_ref[...]).astype(BF16)


def joint_forward(place, x, gain, shift, bias, pieces, rows, tile=256):
    tokens, features = x.shape
    width = bias.shape[1]
    return pl.pallas_call(
        functools.partial(joint_kernel, rows),
        grid=(tokens // tile,),
        in_specs=[
            SMEM,
            pl.BlockSpec((tile, features), lambda t: (t, 0)),
            whole((1, features)),
            whole((1, features)),
            whole((1, width)),
        ]
        + [ANY] * VIRTUAL,
        out_specs=[
            pl.BlockSpec((tile, width), lambda t: (t, 0)),
            pl.BlockSpec((features, tile), lambda t: (0, t)),
            whole((features, width)),
        ],
        out_shape=[
            jax.ShapeDtypeStruct((tokens, width), BF16),
            jax.ShapeDtypeStruct((features, tokens), BF16),
            jax.ShapeDtypeStruct((features, width), BF16),
        ],
        scratch_shapes=[pltpu.SemaphoreType.DMA((VIRTUAL,))],
        compiler_params=pltpu.CompilerParams(vmem_limit_bytes=48 << 20),
        cost_estimate=pl.CostEstimate(
            flops=2 * tokens * features * width, bytes_accessed=14 << 20, transcendentals=0
        ),
        name="joint_forward",
    )(place, x, gain, shift, bias, *pieces)


def attention_forward_kernel(q_ref, k_ref, v_ref, segq_ref, segk_ref, mixed_ref, total_ref):
    queries = q_ref[...] * jnp.asarray(0.125, BF16)
    keys = k_ref[...]
    values_t = v_ref[...].T
    allowed = segk_ref[...] == segq_ref[...]
    lane = lax.broadcasted_iota(jnp.int32, queries.shape, 1)
    mixed, totals = [], []
    for h in range(2):
        mine = jnp.where((lane // HEAD) == h, queries, jnp.zeros_like(queries))
        scores = jnp.where(allowed, dot_nt(keys, mine), -1e30)
        top = jnp.max(scores, axis=0, keepdims=True)
        weights = jnp.exp(scores - top)
        total = jnp.sum(weights, axis=0, keepdims=True)
        probs = (weights * (1.0 / total)).astype(BF16)
        mixed.append(dot_nn(values_t[h * HEAD : (h + 1) * HEAD], probs))
        totals.append(top + jnp.log(total))
    mixed_ref[...] = jnp.concatenate(mixed, axis=0).T.astype(BF16)
    totals.append(jnp.zeros((6,) + totals[0].shape[1:], F32))
    total_ref[0] = jnp.concatenate(totals, axis=0)


def attention_forward(proj, seg_row, seg_column, tile=256):
    tokens, width = proj.shape
    features = width // 3
    pairs = features // PAIR
    return pl.pallas_call(
        attention_forward_kernel,
        grid=(pairs, tokens // tile),
        in_specs=[
            pl.BlockSpec((tile, PAIR), lambda h, i: (i, h)),
            pl.BlockSpec((tokens, PAIR), lambda h, i: (0, pairs + h)),
            pl.BlockSpec((tokens, PAIR), lambda h, i: (0, 2 * pairs + h)),
            pl.BlockSpec((1, tile), lambda h, i: (0, i)),
            whole((tokens, 1)),
        ],
        out_specs=[
            pl.BlockSpec((tile, PAIR), lambda h, i: (i, h)),
            pl.BlockSpec((1, 8, tile), lambda h, i: (h, 0, i)),
        ],
        out_shape=[
            jax.ShapeDtypeStruct((tokens, features), BF16),
            jax.ShapeDtypeStruct((pairs, 8, tokens), F32),
        ],
        compiler_params=pltpu.CompilerParams(vmem_limit_bytes=48 << 20),
        cost_estimate=pl.CostEstimate(
            flops=16 * tokens * tokens * features,
            bytes_accessed=8 << 20,
            transcendentals=tokens * tokens * features // HEAD,
        ),
        name="attention_forward",
    )(proj, proj, proj, seg_row, seg_column)


def attention_backward_kernel(
    q_tiles, q_ref, k_ref, v_ref, g_ref, segq_ref, segk_ref, total_ref, dq_ref, dk_ref, dv_ref, dk_sum, dv_sum
):
    step = pl.program_id(1)
    queries = q_ref[...] * jnp.asarray(0.125, BF16)
    keys, values, grads = k_ref[...], v_ref[...], g_ref[...]
    keys_t = keys.T
    allowed = segk_ref[...] == segq_ref[...]
    lane = lax.broadcasted_iota(jnp.int32, queries.shape, 1)
    grad_q, grad_k, grad_v = [], 0.0, 0.0
    for h in range(2):
        mine = (lane // HEAD) == h
        query = jnp.where(mine, queries, jnp.zeros_like(queries))
        grad = jnp.where(mine, grads, jnp.zeros_like(grads))
        scores = jnp.where(allowed, dot_nt(keys, query), -1e30)
        probs = jnp.exp(scores - total_ref[0, h : h + 1, :])
        grad_probs = dot_nt(values, grad)
        centre = jnp.sum(probs * grad_probs, axis=0, keepdims=True)
        grad_scores = (probs * (grad_probs - centre)).astype(BF16)
        grad_v += dot_nn(probs.astype(BF16), grad)
        grad_k += dot_nn(grad_scores, query)
        grad_q.append(dot_nn(keys_t[h * HEAD : (h + 1) * HEAD], grad_scores))
    dq_ref[...] = (jnp.concatenate(grad_q, axis=0).T * 0.125).astype(BF16)
    accumulate(step, dk_sum, grad_k)
    accumulate(step, dv_sum, grad_v)

    @pl.when(step == q_tiles - 1)
    def _():
        dk_ref[...] = dk_sum[...].astype(BF16)
        dv_ref[...] = dv_sum[...].astype(BF16)


def attention_backward(proj, grad_mixed, seg_row, seg_column, totals, tile=256):
    tokens, width = proj.shape
    features = width // 3
    pairs = features // PAIR
    q_tiles = tokens // tile
    return pl.pallas_call(
        functools.partial(attention_backward_kernel, q_tiles),
        grid=(pairs, q_tiles),
        in_specs=[
            pl.BlockSpec((tile, PAIR), lambda h, i: (i, h)),
            pl.BlockSpec((tokens, PAIR), lambda h, i: (0, pairs + h)),
            pl.BlockSpec((tokens, PAIR), lambda h, i: (0, 2 * pairs + h)),
            pl.BlockSpec((tile, PAIR), lambda h, i: (i, h)),
            pl.BlockSpec((1, tile), lambda h, i: (0, i)),
            whole((tokens, 1)),
            pl.BlockSpec((1, 8, tile), lambda h, i: (h, 0, i)),
        ],
        out_specs=[
            pl.BlockSpec((tile, PAIR), lambda h, i: (i, h)),
            pl.BlockSpec((tokens, PAIR), lambda h, i: (0, h)),
            pl.BlockSpec((tokens, PAIR), lambda h, i: (0, h)),
        ],
        out_shape=[jax.ShapeDtypeStruct((tokens, features), BF16)] * 3,
        scratch_shapes=[pltpu.VMEM((tokens, PAIR), F32)] * 2,
        compiler_params=pltpu.CompilerParams(vmem_limit_bytes=56 << 20),
        cost_estimate=pl.CostEstimate(
            flops=24 * tokens * tokens * features,
            bytes_accessed=14 << 20,
            transcendentals=tokens * tokens * features // HEAD,
        ),
        name="attention_backward",
    )(proj, proj, proj, grad_mixed, seg_row, seg_column, totals)


def middle_kernel(rows, images, place_ref, flags_ref, mixed_ref, x_ref, cot_ref, seg_ref, bias_ref, gain_ref, shift_ref, *refs):
    pieces = refs[:VIRTUAL]
    middle_ref, normed_ref, normed_t_ref, grad_ref, weight_ref, sems = refs[VIRTUAL:]
    features = x_ref.shape[1]

    @pl.when(pl.program_id(0) == 0)
    def _():
        copies = []
        for k in range(VIRTUAL):
            start = pl.multiple_of((place_ref[0] ^ k) * rows, 16)
            copies.append(
                pltpu.make_async_copy(
                    pieces[k].at[:, pl.ds(0, features)],
                    weight_ref.at[pl.ds(start, rows)],
                    sems.at[k],
                )
            )
        for copy in copies:
            copy.start()
        for copy in copies:
            copy.wait()

    branch = dot_nn(mixed_ref[...], weight_ref[...]) + bias_ref[...]
    segment = seg_ref[...]
    middle = x_ref[...].astype(F32) + branch_scale(segment, flags_ref, 0, images) * branch
    middle_ref[...] = middle
    normal, _ = norm_parts(middle)
    normed = (normal * gain_ref[...] + shift_ref[...]).astype(BF16)
    normed_ref[...] = normed
    normed_t_ref[...] = normed.T
    mlp_scale = branch_scale(segment, flags_ref, images, images)
    grad_ref[...] = (mlp_scale * cot_ref[...].astype(F32)).astype(BF16)


def middle_forward(place, flags, mixed, x, cot, seg_column, bias, gain, shift, pieces, rows, tile=256):
    tokens, features = x.shape
    images = flags.shape[0] // 2
    row_block = pl.BlockSpec((tile, features), lambda t: (t, 0))
    return pl.pallas_call(
        functools.partial(middle_kernel, rows, images),
        grid=(tokens // tile,),
        in_specs=[SMEM, SMEM, row_block, row_block, row_block, pl.BlockSpec((tile, 1), lambda t: (t, 0))]
        + [whole((1, features))] * 3
        + [ANY] * VIRTUAL,
        out_specs=[
            row_block,
            row_block,
            pl.BlockSpec((features, tile), lambda t: (0, t)),
            row_block,
            whole((features, features)),
        ],
        out_shape=[
            jax.ShapeDtypeStruct((tokens, features), F32),
            jax.ShapeDtypeStruct((tokens, features), BF16),
            jax.ShapeDtypeStruct((features, tokens), BF16),
            jax.ShapeDtypeStruct((tokens, features), BF16),
            jax.ShapeDtypeStruct((features, features), BF16),
        ],
        scratch_shapes=[pltpu.SemaphoreType.DMA((VIRTUAL,))],
        compiler_params=pltpu.CompilerParams(vmem_limit_bytes=48 << 20),
        cost_estimate=pl.CostEstimate(
            flops=2 * tokens * features * features, bytes_accessed=16 << 20, transcendentals=0
        ),
        name="middle_forward",
    )(place, flags, mixed, x, cot, seg_column, bias, gain, shift, *pieces)


def split_shards(rows, place, source_ref, keep_ref, send_ref):
    for pair in range(VIRTUAL // 2):
        slot = pair ^ (place >> 1)
        stay = pl.multiple_of((2 * pair + (place & 1)) * rows, 16)
        leave = pl.multiple_of((2 * pair + 1 - (place & 1)) * rows, 16)
        keep_ref[slot] = source_ref[pl.ds(stay, rows), :]
        send_ref[slot] = source_ref[pl.ds(leave, rows), :]


root_half = 0.7071067811865476
root_two_pi_inverse = 0.3989422804014327


def mlp_kernel(rows, tiles, block, place_ref, normed_ref, normed_t_ref, g_ref, bias_ref, *refs):
    pieces = refs[:VIRTUAL]
    (out_ref, gn_ref, keep1_ref, send1_ref, keep2_ref, send2_ref, db_ref) = refs[VIRTUAL : VIRTUAL + 7]
    w1_s, w2_s, act_s, gp_s, dw_s, sems = refs[VIRTUAL + 7 :]
    f = pl.program_id(0)
    place = place_ref[0]
    tokens, features = normed_ref.shape
    hidden = w1_s.shape[1]
    parts = hidden // features

    @pl.when(f == 0)
    def _():
        copies = []
        for k in range(VIRTUAL):
            start = pl.multiple_of((place ^ k) * rows, 16)
            copies.append(
                pltpu.make_async_copy(
                    pieces[k].at[:, pl.ds(features, hidden)], w1_s.at[pl.ds(start, rows)], sems.at[0, k]
                )
            )
            for part in range(parts):
                start = pl.multiple_of(((place ^ k) * parts + part) * rows, 16)
                copies.append(
                    pltpu.make_async_copy(
                        pieces[k].at[:, pl.ds(features + hidden + part * features, features)],
                        w2_s.at[pl.ds(start, rows)],
                        sems.at[1 + part, k],
                    )
                )
        for copy in copies:
            copy.start()
        for copy in copies:
            copy.wait()

    first = pl.multiple_of(f * block, block)
    w1 = w1_s[:, pl.ds(first, block)]
    w2 = w2_s[pl.ds(first, block), :]
    bias = bias_ref[...]
    step = tokens // tiles
    db = jnp.zeros((1, block), F32)
    for t in range(tiles):
        part = slice(t * step, (t + 1) * step)
        pre = dot_nn(normed_ref[part, :], w1) + bias
        cdf = 0.5 * (1.0 + lax.erf(pre * root_half))
        act = (pre * cdf).astype(BF16)
        slope = cdf + pre * (jnp.exp(-0.5 * pre * pre) * root_two_pi_inverse)
        gp = (dot_nt(g_ref[part, :], w2) * slope).astype(BF16)
        db += jnp.sum(gp.astype(F32), axis=0, keepdims=True)
        act_s[part, :] = act
        gp_s[part, :] = gp
        out = dot_nn(act, w2)
        gn = dot_nt(gp, w1)

        @pl.when(f == 0)
        def _():
            out_ref[part, :] = out
            gn_ref[part, :] = gn

        @pl.when(f > 0)
        def _():
            out_ref[part, :] += out
            gn_ref[part, :] += gn

    db_ref[...] = db
    dw_s[...] = dot_nn(normed_t_ref[...], gp_s[...]).astype(BF16)
    split_shards(rows, place, dw_s, keep1_ref, send1_ref)
    dw_s[...] = dot_tn(act_s[...], g_ref[...]).astype(BF16)
    slot = f ^ (place >> 1)
    for part in range(parts):
        stay = pl.multiple_of(((place & 1) * parts + part) * rows, 16)
        leave = pl.multiple_of(((1 - (place & 1)) * parts + part) * rows, 16)
        columns = slice(part * features, (part + 1) * features)
        keep2_ref[slot, :, columns] = dw_s[pl.ds(stay, rows), :]
        send2_ref[slot, :, columns] = dw_s[pl.ds(leave, rows), :]


def mlp(place, normed, normed_t, grads, bias, pieces, rows, tiles=4):
    tokens, features = normed.shape
    hidden = bias.shape[1]
    parts = hidden // features
    block = 2 * hidden // VIRTUAL
    assert block == features
    half = VIRTUAL // 2
    columns = pl.BlockSpec((half, rows, block), lambda f: (0, 0, f))
    shards = jax.ShapeDtypeStruct((half, rows, hidden), BF16)
    return pl.pallas_call(
        functools.partial(mlp_kernel, rows, tiles, block),
        grid=(hidden // block,),
        in_specs=[
            SMEM,
            whole((tokens, features)),
            whole((features, tokens)),
            whole((tokens, features)),
            pl.BlockSpec((1, block), lambda f: (0, f)),
        ]
        + [ANY] * VIRTUAL,
        out_specs=[
            whole((tokens, features)),
            whole((tokens, features)),
            columns,
            columns,
            whole((half, rows, hidden)),
            whole((half, rows, hidden)),
            pl.BlockSpec((1, block), lambda f: (0, f)),
        ],
        out_shape=[jax.ShapeDtypeStruct((tokens, features), F32)] * 2
        + [shards] * 4
        + [jax.ShapeDtypeStruct((1, hidden), F32)],
        scratch_shapes=[
            pltpu.VMEM((features, hidden), BF16),
            pltpu.VMEM((hidden, features), BF16),
            pltpu.VMEM((tokens, block), BF16),
            pltpu.VMEM((tokens, block), BF16),
            pltpu.VMEM((features, block), BF16),
            pltpu.SemaphoreType.DMA((1 + parts, VIRTUAL)),
        ],
        compiler_params=pltpu.CompilerParams(vmem_limit_bytes=62 << 20),
        cost_estimate=pl.CostEstimate(
            flops=12 * tokens * features * hidden,
            bytes_accessed=30 << 20,
            transcendentals=2 * tokens * hidden,
        ),
        name="mlp",
    )(place, normed, normed_t, grads, bias, *pieces)


def output_backward_kernel(
    rows, images, steps, place_ref, flags_ref, middle_ref, gn_ref, branch_ref, cot_ref, mixed_ref, seg_ref,
    gain_ref, bias_ref, weight_ref, out_ref, gm_ref, gx_ref, keep_ref, send_ref, sums_ref, dw_sum, dw_s,
):
    step = pl.program_id(0)
    segment = seg_ref[...]
    attn_scale = branch_scale(segment, flags_ref, 0, images)
    mlp_scale = branch_scale(segment, flags_ref, images, images)
    middle = middle_ref[...]
    cot = cot_ref[...].astype(F32)
    out_ref[...] = (middle + mlp_scale * (branch_ref[...] + bias_ref[...])).astype(BF16)
    grad_b = (mlp_scale * cot).astype(BF16)
    gn = gn_ref[...]
    normal, inverse = norm_parts(middle)
    grad_middle = cot + norm_backward(normal, inverse, gn, gain_ref[...])
    gm_ref[...] = grad_middle
    grad_a = (attn_scale * grad_middle).astype(BF16)
    gx_ref[...] = dot_nt(grad_a, weight_ref[...]).astype(BF16)
    accumulate(step, dw_sum, dot_tn(mixed_ref[...], grad_a))
    total = lambda v: jnp.sum(v, axis=0, keepdims=True)
    sums = [total(gn * normal), total(gn), total(grad_a.astype(F32)), total(grad_b.astype(F32))]
    accumulate(step, sums_ref, jnp.concatenate(sums + [jnp.zeros((4,) + sums[0].shape[1:], F32)], axis=0))

    @pl.when(step == steps - 1)
    def _():
        dw_s[...] = dw_sum[...].astype(BF16)
        split_shards(rows, place_ref[0], dw_s, keep_ref, send_ref)


def output_backward(place, flags, middle, gn, branch, cot, mixed, seg_column, gain, bias, weight, rows, tile=256):
    tokens, features = middle.shape
    images = flags.shape[0] // 2
    half = VIRTUAL // 2
    steps = tokens // tile
    row_block = pl.BlockSpec((tile, features), lambda t: (t, 0))
    shards = jax.ShapeDtypeStruct((half, rows, features), BF16)
    return pl.pallas_call(
        functools.partial(output_backward_kernel, rows, images, steps),
        grid=(steps,),
        in_specs=[SMEM, SMEM]
        + [row_block] * 5
        + [pl.BlockSpec((tile, 1), lambda t: (t, 0)), whole((1, features)), whole((1, features)), whole((features, features))],
        out_specs=[row_block, row_block, row_block, whole((half, rows, features)), whole((half, rows, features)), whole((8, features))],
        out_shape=[
            jax.ShapeDtypeStruct((tokens, features), BF16),
            jax.ShapeDtypeStruct((tokens, features), F32),
            jax.ShapeDtypeStruct((tokens, features), BF16),
            shards,
            shards,
            jax.ShapeDtypeStruct((8, features), F32),
        ],
        scratch_shapes=[pltpu.VMEM((features, features), F32), pltpu.VMEM((features, features), BF16)],
        compiler_params=pltpu.CompilerParams(vmem_limit_bytes=56 << 20),
        cost_estimate=pl.CostEstimate(
            flops=4 * tokens * features * features, bytes_accessed=22 << 20, transcendentals=0
        ),
        name="output_backward",
    )(place, flags, middle, gn, branch, cot, mixed, seg_column, gain, bias, weight)


def joint_weight_kernel(rows, place_ref, normed_t_ref, dq_ref, dk_ref, dv_ref, keep_ref, send_ref, sums_ref, dw_s):
    step = pl.program_id(0)

    def block(ref):
        grads = ref[...]
        dw_s[...] = dot_nn(normed_t_ref[...], grads).astype(BF16)
        sums_ref[...] = jnp.sum(grads.astype(F32), axis=0, keepdims=True)

    for index, ref in enumerate((dq_ref, dk_ref, dv_ref)):
        pl.when(step == index)(functools.partial(block, ref))
    split_shards(rows, place_ref[0], dw_s, keep_ref, send_ref)


def joint_weight_grad(place, normed_t, dq, dk, dv, rows):
    features, tokens = normed_t.shape
    half = VIRTUAL // 2
    columns = pl.BlockSpec((half, rows, features), lambda c: (0, 0, c))
    shards = jax.ShapeDtypeStruct((half, rows, 3 * features), BF16)
    return pl.pallas_call(
        functools.partial(joint_weight_kernel, rows),
        grid=(3,),
        in_specs=[SMEM, whole((features, tokens))] + [whole((tokens, features))] * 3,
        out_specs=[columns, columns, pl.BlockSpec((1, features), lambda c: (0, c))],
        out_shape=[shards, shards, jax.ShapeDtypeStruct((1, 3 * features), F32)],
        scratch_shapes=[pltpu.VMEM((features, features), BF16)],
        compiler_params=pltpu.CompilerParams(vmem_limit_bytes=48 << 20),
        cost_estimate=pl.CostEstimate(
            flops=6 * tokens * features * features, bytes_accessed=10 << 20, transcendentals=0
        ),
        name="joint_weight_grad",
    )(place, normed_t, dq, dk, dv)


def joint_backward_kernel(dq_ref, dk_ref, dv_ref, weight_ref, x_ref, gm_ref, gain_ref, gt_ref, sums_ref):
    features = x_ref.shape[1]
    gn = dot_nt(dq_ref[...], weight_ref[:, :features])
    gn += dot_nt(dk_ref[...], weight_ref[:, features : 2 * features])
    gn += dot_nt(dv_ref[...], weight_ref[:, 2 * features :])
    normal, inverse = norm_parts(x_ref[...].astype(F32))
    gt_ref[...] = (gm_ref[...] + norm_backward(normal, inverse, gn, gain_ref[...])).astype(BF16)
    total = lambda v: jnp.sum(v, axis=0, keepdims=True)
    sums = [total(gn * normal), total(gn)]
    accumulate(
        pl.program_id(0), sums_ref, jnp.concatenate(sums + [jnp.zeros((6, features), F32)], axis=0)
    )


def joint_backward(dq, dk, dv, weight, x, gm, gain, tile=256):
    tokens, features = x.shape
    row_block = pl.BlockSpec((tile, features), lambda t: (t, 0))
    return pl.pallas_call(
        joint_backward_kernel,
        grid=(tokens // tile,),
        in_specs=[row_block] * 3 + [whole((features, 3 * features)), row_block, row_block, whole((1, features))],
        out_specs=[row_block, whole((8, features))],
        out_shape=[jax.ShapeDtypeStruct((tokens, features), BF16), jax.ShapeDtypeStruct((8, features), F32)],
        compiler_params=pltpu.CompilerParams(vmem_limit_bytes=48 << 20),
        cost_estimate=pl.CostEstimate(
            flops=6 * tokens * features * features, bytes_accessed=15 << 20, transcendentals=0
        ),
        name="joint_backward",
    )(dq, dk, dv, weight, x, gm, gain)


def after(value, *others):
    return lax.optimization_barrier((value,) + others)[0]


def dp_swap(value, bit):
    return lax.ppermute(value, "dp", [(i, i ^ bit) for i in range(VIRTUAL)])


def seq_exchange(value, parts):
    me = lax.axis_index("seq")

    def block(place):
        return lax.dynamic_index_in_dim(value, place % parts, 0, keepdims=False)

    order = sorted(range(1, parts), key=lambda k: abs(k - parts / 2))
    got = [
        (k, lax.ppermute(block(me + k), "seq", [(i, (i + k) % parts) for i in range(parts)]))
        for k in order
    ]
    out = lax.dynamic_update_index_in_dim(jnp.zeros_like(value), block(me), me, 0)
    for k, arrived in got:
        out = lax.dynamic_update_index_in_dim(out, arrived, (me - k) % parts, 0)
    return out


def gather_shards(own, first):
    far_x, far_y = dp_swap(own, 2), dp_swap(own, 4)
    corner = dp_swap(far_x, 4) if first == 2 else dp_swap(far_y, 2)
    mine = (own, far_x, far_y, corner)
    other = [dp_swap(piece, 1) for piece in mine]
    return [piece for both in zip(mine, other) for piece in both]


def add(left, right):
    return left.astype(F32) + right.astype(F32)


def scatter_rest(half, first):
    if first == 2:
        one = add(half[0::2], dp_swap(half[1::2], 2)).astype(BF16)
        return add(one[0], dp_swap(one[1], 4))
    one = add(half[:2], dp_swap(half[2:], 4)).astype(BF16)
    return add(one[0], dp_swap(one[1], 2))


def seq_sum(value, parts):
    rows = value.shape[0] // parts
    cut = value.astype(BF16).reshape(parts, rows, value.shape[1])
    arrived = seq_exchange(cut, parts)
    total = jnp.sum(arrived.astype(F32), axis=0).astype(BF16)
    me = lax.axis_index("seq")
    out = lax.dynamic_update_index_in_dim(jnp.zeros_like(cut), total, me, 0)
    for k in range(1, parts):
        got = lax.ppermute(total, "seq", [(i, (i + k) % parts) for i in range(parts)])
        out = lax.dynamic_update_index_in_dim(out, got, (me - k) % parts, 0)
    return out.astype(F32).reshape(value.shape)


def sum_everywhere(value, parts):
    for bit in (1, 2, 4):
        value = value + dp_swap(value, bit)
    if parts & (parts - 1):
        return lax.psum(value, "seq")
    bit = 1
    while bit < parts:
        value = value + lax.ppermute(value, "seq", [(i, i ^ bit) for i in range(parts)])
        bit *= 2
    return value


def pack_rows(matrix, rows):
    groups = matrix.shape[0] // rows
    return jnp.concatenate([matrix[g * rows : (g + 1) * rows] for g in range(groups)], axis=1)


def unpack_rows(matrix, features):
    groups = matrix.shape[1] // features
    return jnp.concatenate([matrix[:, g * features : (g + 1) * features] for g in range(groups)], axis=0)


def shards(
    ndp,
    nseq,
    tokens,
    cotangent,
    segments,
    keep_flags,
    first_gain,
    first_shift,
    joint_weight,
    joint_bias,
    output_weight,
    output_bias,
    second_gain,
    second_shift,
    expand_weight,
    expand_bias,
    reduce_weight,
    reduce_bias,
):
    row_count, shard_len, features = tokens.shape
    assert row_count == nseq
    row_len = segments.shape[1]
    hidden = expand_weight.shape[1]
    rows = features // VIRTUAL
    me_seq = lax.axis_index("seq")
    me_dp = lax.axis_index("dp")
    exact = ndp == VIRTUAL

    smalls = (first_gain, first_shift, joint_bias, output_bias, second_gain, second_shift, expand_bias, reduce_bias)
    widths = [s.shape[0] * ndp for s in smalls]

    x = seq_exchange(tokens, nseq).reshape(row_len, features)

    if exact:
        place = me_dp.astype(jnp.int32).reshape(1)
        row = jnp.concatenate([s.astype(BF16) for s in smalls])
        width = 3 * features
        row = jnp.pad(row, (0, width - row.shape[0])).reshape(1, width)
        piece = jnp.concatenate([joint_weight.astype(BF16), jnp.pad(row, ((0, 15), (0, 0)))], axis=0)
        joint_pieces = gather_shards(piece, 2)
        small_slots = jnp.stack([p[rows, : sum(w // ndp for w in widths)] for p in joint_pieces]).astype(F32)
        slot = lax.broadcasted_iota(jnp.int32, (VIRTUAL, VIRTUAL, 1), 1)
        home = lax.broadcasted_iota(jnp.int32, (VIRTUAL, VIRTUAL, 1), 0)
        ordered = jnp.sum(jnp.where(slot == (home ^ me_dp), small_slots[None], 0.0), axis=1)
        params, start = [], 0
        for w in widths:
            params.append(ordered[:, start : start + w // ndp].reshape(1, w))
            start += w // ndp
        piece = jnp.concatenate(
            [output_weight.astype(BF16), expand_weight.astype(BF16), pack_rows(reduce_weight.astype(BF16), rows)],
            axis=1,
        )
        piece = after(piece, joint_pieces[2], joint_pieces[4])
        rest_pieces = gather_shards(piece, 4)
    else:
        place = jnp.zeros((1,), jnp.int32)
        full = lambda w: lax.all_gather(w.astype(BF16), "dp", axis=0, tiled=True)
        params = [full(s).astype(F32).reshape(1, -1) for s in smalls]
        joint = full(joint_weight)
        out_w, up_w, down_w = full(output_weight), full(expand_weight), full(reduce_weight)
        joint_pieces = [joint[k * rows : (k + 1) * rows] for k in range(VIRTUAL)]
        group = hidden // VIRTUAL
        rest_pieces = [
            jnp.concatenate(
                [
                    out_w[k * rows : (k + 1) * rows],
                    up_w[k * rows : (k + 1) * rows],
                    pack_rows(down_w[k * group : (k + 1) * group], rows),
                ],
                axis=1,
            )
            for k in range(VIRTUAL)
        ]
    gain_a, shift_a, bias_qv, bias_out, gain_b, shift_b, bias_up, bias_down = params
    bias_joint = jnp.concatenate([bias_qv[:, :features], jnp.zeros((1, features), F32), bias_qv[:, features:]], axis=1)

    seg = lax.dynamic_index_in_dim(segments, me_seq, 0, keepdims=False)
    flags = lax.dynamic_index_in_dim(keep_flags, me_seq, 0, keepdims=False)
    seg_row, seg_column = seg.reshape(1, row_len), seg.reshape(row_len, 1)

    cot = seq_exchange(after(cotangent, x), nseq).reshape(row_len, features)

    proj, normed_a_t, weight_joint = joint_forward(place, x, gain_a, shift_a, bias_joint, joint_pieces, rows)
    mixed, totals = attention_forward(proj, seg_row, seg_column)
    middle, normed_b, normed_b_t, grad_b, weight_out = middle_forward(
        place, flags, mixed, x, cot, seg_column, bias_out, gain_b, shift_b, rest_pieces, rows
    )
    branch, gn, keep_up, send_up, keep_down, send_down, g_bias_up = mlp(
        place, normed_b, normed_b_t, grad_b, bias_up, rest_pieces, rows
    )
    output, grad_middle, grad_mixed, keep_out, send_out, sums_b = output_backward(
        place, flags, middle, gn, branch, cot, mixed, seg_column, gain_b, bias_down, weight_out, rows
    )
    dq, dk, dv = attention_backward(proj, grad_mixed, seg_row, seg_column, totals)
    keep_joint, send_joint, sums_joint = joint_weight_grad(place, normed_a_t, dq, dk, dv, rows)
    grad_in, sums_a = joint_backward(dq, dk, dv, weight_joint, x, grad_middle, gain_a)

    output = seq_exchange(output.reshape(nseq, shard_len, features), nseq)
    grad_tokens = seq_exchange(grad_in.reshape(nseq, shard_len, features), nseq).astype(F32)

    late = jnp.concatenate([sums_a[0], sums_a[1], sums_joint[0, :features], sums_joint[0, 2 * features :]])
    early = jnp.concatenate([sums_b[2], sums_b[0], sums_b[1], g_bias_up[0], sums_b[3]])
    if exact:
        early = sum_everywhere(early.reshape(-1, 128), nseq).reshape(-1)
        late = sum_everywhere(late.reshape(-1, 128), nseq).reshape(-1)
        half_up = add(keep_up, dp_swap(send_up, 1)).astype(BF16)
        half_down = add(keep_down, dp_swap(send_down, 1)).astype(BF16)
        half_out = add(keep_out, dp_swap(send_out, 1)).astype(BF16)
        first = jnp.concatenate(
            [scatter_rest(half_up, 2), scatter_rest(half_down, 4), scatter_rest(half_out, 2)], axis=1
        )
        first = seq_sum(first, nseq)
        g_up = first[:, :hidden]
        g_down = unpack_rows(first[:, hidden : 2 * hidden], features)
        g_out = first[:, 2 * hidden :]
        arrived = dp_swap(send_joint, 1)
        cut = 3 * features // 2
        half_a = add(keep_joint[:, :, :cut], arrived[:, :, :cut]).astype(BF16)
        half_b = add(keep_joint[:, :, cut:], arrived[:, :, cut:]).astype(BF16)
        g_joint = seq_sum(jnp.concatenate([scatter_rest(half_a, 2), scatter_rest(half_b, 4)], axis=1), nseq)
    else:
        early, late = lax.psum((early, late), ("dp", "seq"))

        def total(keep, send):
            return jnp.stack([keep, send], axis=1).reshape(features, keep.shape[2])

        def reduce(matrix):
            part = lax.psum_scatter(matrix.astype(F32), "dp", scatter_dimension=0, tiled=True)
            return lax.psum(part, "seq")

        g_up = reduce(total(keep_up, send_up))
        g_out = reduce(total(keep_out, send_out))
        g_joint = reduce(total(keep_joint, send_joint))
        down = jnp.stack([keep_down, send_down], axis=1).reshape(VIRTUAL, rows, hidden)
        g_down = reduce(jnp.concatenate([unpack_rows(down[k], features) for k in range(VIRTUAL)], axis=0))

    def mine(vector, start, size):
        piece = size // ndp
        return lax.dynamic_slice_in_dim(vector, start + me_dp * piece, piece, 0)

    g_first_gain = mine(late, 0, features)
    g_first_shift = mine(late, features, features)
    g_joint_bias = mine(late, 2 * features, 2 * features)
    g_output_bias = mine(early, 0, features)
    g_second_gain = mine(early, features, features)
    g_second_shift = mine(early, 2 * features, features)
    g_expand_bias = mine(early, 3 * features, hidden)
    g_reduce_bias = mine(early, 3 * features + hidden, features)
    return (
        output,
        grad_tokens,
        g_first_gain,
        g_first_shift,
        g_joint,
        g_joint_bias,
        g_out,
        g_output_bias,
        g_second_gain,
        g_second_shift,
        g_up,
        g_expand_bias,
        g_down,
        g_reduce_bias,
    )


def solution(mesh):
    vector, matrix = P("dp"), P("dp", None)
    token_spec = P("dp", "seq", None)
    params = (vector, vector, matrix, vector, matrix, vector, vector, vector, matrix, vector, matrix, vector)
    return jax.shard_map(
        functools.partial(shards, mesh.shape["dp"], mesh.shape["seq"]),
        mesh=mesh,
        in_specs=(token_spec, token_spec, matrix, matrix) + params,
        out_specs=(token_spec, token_spec) + params,
        check_vma=False,
    )
```

```python
import functools

import jax
import jax.numpy as jnp
from jax import lax
from jax.experimental import pallas as pl
from jax.experimental.pallas import tpu as pltpu
from jax.sharding import PartitionSpec as P

HEAD = 64
PAIR = 2 * HEAD
VIRTUAL = 8
keep_ratio_inverse = 1.0 / 0.9
norm_epsilon = 1e-06
F32 = jnp.float32
BF16 = jnp.bfloat16


def dot_nn(left, right):
    return lax.dot_general(left, right, (((1,), (0,)), ((), ())), preferred_element_type=F32)


def dot_nt(left, right):
    return lax.dot_general(left, right, (((1,), (1,)), ((), ())), preferred_element_type=F32)


def dot_tn(left, right):
    return lax.dot_general(left, right, (((0,), (0,)), ((), ())), preferred_element_type=F32)


def whole(shape):
    return pl.BlockSpec(shape, lambda *_: (0,) * len(shape))


def once(shape):
    return pl.BlockSpec(shape, lambda *_: (0,) * len(shape), pipeline_mode=pl.Buffered(1))


SMEM = pl.BlockSpec(memory_space=pltpu.SMEM)
ANY = pl.BlockSpec(memory_space=pl.ANY)


def branch_scale(segment_column, flags_ref, first, images):
    scale = jnp.zeros(segment_column.shape, F32)
    for image in range(images):
        flag = flags_ref[first + image].astype(F32) * keep_ratio_inverse
        scale = jnp.where(segment_column == image, flag, scale)
    return scale


def norm_parts(inputs):
    centre = inputs - jnp.mean(inputs, axis=-1, keepdims=True)
    spread = jnp.mean(centre * centre, axis=-1, keepdims=True)
    inverse = lax.rsqrt(spread + norm_epsilon)
    return centre * inverse, inverse


def norm_backward(normal, inverse, grads, gain):
    scaled = grads * gain
    mean_scaled = jnp.mean(scaled, axis=-1, keepdims=True)
    mean_product = jnp.mean(scaled * normal, axis=-1, keepdims=True)
    return (scaled - mean_scaled - normal * mean_product) * inverse


def accumulate(step, ref, value):
    @pl.when(step == 0)
    def _():
        ref[...] = value

    @pl.when(step > 0)
    def _():
        ref[...] += value


def joint_kernel(rows, place_ref, x_ref, gain_ref, shift_ref, bias_ref, *refs):
    pieces = refs[:VIRTUAL]
    proj_ref, normed_t_ref, weight_ref, sems = refs[VIRTUAL:]

    @pl.when(pl.program_id(0) == 0)
    def _():
        copies = []
        for k in range(VIRTUAL):
            start = pl.multiple_of((place_ref[0] ^ k) * rows, 16)
            copies.append(
                pltpu.make_async_copy(
                    pieces[k].at[pl.ds(0, rows)], weight_ref.at[pl.ds(start, rows)], sems.at[k]
                )
            )
        for copy in copies:
            copy.start()
        for copy in copies:
            copy.wait()

    normal, _ = norm_parts(x_ref[...].astype(F32))
    normed = (normal * gain_ref[...] + shift_ref[...]).astype(BF16)
    normed_t_ref[...] = normed.T
    proj_ref[...] = (dot_nn(normed, weight_ref[...]) + bias_ref[...]).astype(BF16)


def joint_forward(place, x, gain, shift, bias, pieces, rows, tile=256):
    tokens, features = x.shape
    width = bias.shape[1]
    return pl.pallas_call(
        functools.partial(joint_kernel, rows),
        grid=(tokens // tile,),
        in_specs=[
            SMEM,
            pl.BlockSpec((tile, features), lambda t: (t, 0)),
            whole((1, features)),
            whole((1, features)),
            whole((1, width)),
        ]
        + [ANY] * VIRTUAL,
        out_specs=[
            pl.BlockSpec((tile, width), lambda t: (t, 0)),
            pl.BlockSpec((features, tile), lambda t: (0, t)),
            whole((features, width)),
        ],
        out_shape=[
            jax.ShapeDtypeStruct((tokens, width), BF16),
            jax.ShapeDtypeStruct((features, tokens), BF16),
            jax.ShapeDtypeStruct((features, width), BF16),
        ],
        scratch_shapes=[pltpu.SemaphoreType.DMA((VIRTUAL,))],
        compiler_params=pltpu.CompilerParams(vmem_limit_bytes=48 << 20),
        cost_estimate=pl.CostEstimate(
            flops=2 * tokens * features * width, bytes_accessed=14 << 20, transcendentals=0
        ),
        name="joint_forward",
    )(place, x, gain, shift, bias, *pieces)


def attention_forward_kernel(q_ref, k_ref, v_ref, segq_ref, segk_ref, mixed_ref, total_ref):
    queries = q_ref[...] * jnp.asarray(0.125, BF16)
    keys = k_ref[...]
    values_t = v_ref[...].T
    allowed = segk_ref[...] == segq_ref[...]
    lane = lax.broadcasted_iota(jnp.int32, queries.shape, 1)
    mixed, totals = [], []
    for h in range(2):
        mine = jnp.where((lane // HEAD) == h, queries, jnp.zeros_like(queries))
        scores = jnp.where(allowed, dot_nt(keys, mine), -1e30)
        top = jnp.max(scores, axis=0, keepdims=True)
        weights = jnp.exp(scores - top)
        total = jnp.sum(weights, axis=0, keepdims=True)
        probs = (weights * (1.0 / total)).astype(BF16)
        mixed.append(dot_nn(values_t[h * HEAD : (h + 1) * HEAD], probs))
        totals.append(top + jnp.log(total))
    mixed_ref[...] = jnp.concatenate(mixed, axis=0).T.astype(BF16)
    totals.append(jnp.zeros((6,) + totals[0].shape[1:], F32))
    total_ref[0] = jnp.concatenate(totals, axis=0)


def attention_forward(proj, seg_row, seg_column, part, parts, tile=256):
    tokens, width = proj.shape
    every = width // 3 // PAIR
    pairs = every // parts
    features = pairs * PAIR
    base = part * pairs
    return pl.pallas_call(
        attention_forward_kernel,
        grid=(pairs, tokens // tile),
        in_specs=[
            pl.BlockSpec((tile, PAIR), lambda h, i: (i, base + h)),
            pl.BlockSpec((tokens, PAIR), lambda h, i: (0, every + base + h)),
            pl.BlockSpec((tokens, PAIR), lambda h, i: (0, 2 * every + base + h)),
            pl.BlockSpec((1, tile), lambda h, i: (0, i)),
            whole((tokens, 1)),
        ],
        out_specs=[
            pl.BlockSpec((tile, PAIR), lambda h, i: (i, h)),
            pl.BlockSpec((1, 8, tile), lambda h, i: (h, 0, i)),
        ],
        out_shape=[
            jax.ShapeDtypeStruct((tokens, features), BF16),
            jax.ShapeDtypeStruct((pairs, 8, tokens), F32),
        ],
        compiler_params=pltpu.CompilerParams(vmem_limit_bytes=48 << 20),
        cost_estimate=pl.CostEstimate(
            flops=16 * tokens * tokens * features,
            bytes_accessed=8 << 20,
            transcendentals=tokens * tokens * features // HEAD,
        ),
        name="attention_forward",
    )(proj, proj, proj, seg_row, seg_column)


def attention_backward_kernel(
    q_tiles, q_ref, k_ref, v_ref, g_ref, segq_ref, segk_ref, total_ref, dq_ref, dk_ref, dv_ref, dk_sum, dv_sum
):
    step = pl.program_id(1)
    queries = q_ref[...] * jnp.asarray(0.125, BF16)
    keys, values, grads = k_ref[...], v_ref[...], g_ref[...]
    keys_t = keys.T
    allowed = segk_ref[...] == segq_ref[...]
    lane = lax.broadcasted_iota(jnp.int32, queries.shape, 1)
    grad_q, grad_k, grad_v = [], 0.0, 0.0
    for h in range(2):
        mine = (lane // HEAD) == h
        query = jnp.where(mine, queries, jnp.zeros_like(queries))
        grad = jnp.where(mine, grads, jnp.zeros_like(grads))
        scores = jnp.where(allowed, dot_nt(keys, query), -1e30)
        probs = jnp.exp(scores - total_ref[0, h : h + 1, :])
        grad_probs = dot_nt(values, grad)
        centre = jnp.sum(probs * grad_probs, axis=0, keepdims=True)
        grad_scores = (probs * (grad_probs - centre)).astype(BF16)
        grad_v += dot_nn(probs.astype(BF16), grad)
        grad_k += dot_nn(grad_scores, query)
        grad_q.append(dot_nn(keys_t[h * HEAD : (h + 1) * HEAD], grad_scores))
    dq_ref[...] = (jnp.concatenate(grad_q, axis=0).T * 0.125).astype(BF16)
    accumulate(step, dk_sum, grad_k)
    accumulate(step, dv_sum, grad_v)

    @pl.when(step == q_tiles - 1)
    def _():
        dk_ref[...] = dk_sum[...].astype(BF16)
        dv_ref[...] = dv_sum[...].astype(BF16)


def attention_backward(proj, grad_mixed, seg_row, seg_column, totals, part, parts, tile=256):
    tokens, width = proj.shape
    every = width // 3 // PAIR
    pairs = every // parts
    features = pairs * PAIR
    base = part * pairs
    q_tiles = tokens // tile
    return pl.pallas_call(
        functools.partial(attention_backward_kernel, q_tiles),
        grid=(pairs, q_tiles),
        in_specs=[
            pl.BlockSpec((tile, PAIR), lambda h, i: (i, base + h)),
            pl.BlockSpec((tokens, PAIR), lambda h, i: (0, every + base + h)),
            pl.BlockSpec((tokens, PAIR), lambda h, i: (0, 2 * every + base + h)),
            pl.BlockSpec((tile, PAIR), lambda h, i: (i, base + h)),
            pl.BlockSpec((1, tile), lambda h, i: (0, i)),
            whole((tokens, 1)),
            pl.BlockSpec((1, 8, tile), lambda h, i: (h, 0, i)),
        ],
        out_specs=[
            pl.BlockSpec((tile, PAIR), lambda h, i: (i, h)),
            pl.BlockSpec((tokens, PAIR), lambda h, i: (0, h)),
            pl.BlockSpec((tokens, PAIR), lambda h, i: (0, h)),
        ],
        out_shape=[jax.ShapeDtypeStruct((tokens, features), BF16)] * 3,
        scratch_shapes=[pltpu.VMEM((tokens, PAIR), F32)] * 2,
        compiler_params=pltpu.CompilerParams(vmem_limit_bytes=56 << 20),
        cost_estimate=pl.CostEstimate(
            flops=24 * tokens * tokens * features,
            bytes_accessed=14 << 20,
            transcendentals=tokens * tokens * features // HEAD,
        ),
        name="attention_backward",
    )(proj, proj, proj, grad_mixed, seg_row, seg_column, totals)


def middle_kernel(rows, images, place_ref, flags_ref, mixed0_ref, mixed1_ref, x_ref, cot_ref, seg_ref, bias_ref, gain_ref, shift_ref, *refs):
    pieces = refs[:VIRTUAL]
    middle_ref, normed_ref, normed_t_ref, grad_ref, weight_ref, sems = refs[VIRTUAL:]
    features = x_ref.shape[1]

    @pl.when(pl.program_id(0) == 0)
    def _():
        copies = []
        for k in range(VIRTUAL):
            start = pl.multiple_of((place_ref[0] ^ k) * rows, 16)
            copies.append(
                pltpu.make_async_copy(
                    pieces[k].at[:, pl.ds(0, features)],
                    weight_ref.at[pl.ds(start, rows)],
                    sems.at[k],
                )
            )
        for copy in copies:
            copy.start()
        for copy in copies:
            copy.wait()

    half = features // 2
    branch = dot_nn(mixed0_ref[...], weight_ref[:half]) + dot_nn(mixed1_ref[...], weight_ref[half:]) + bias_ref[...]
    segment = seg_ref[...]
    middle = x_ref[...].astype(F32) + branch_scale(segment, flags_ref, 0, images) * branch
    middle_ref[...] = middle
    normal, _ = norm_parts(middle)
    normed = (normal * gain_ref[...] + shift_ref[...]).astype(BF16)
    normed_ref[...] = normed
    normed_t_ref[...] = normed.T
    mlp_scale = branch_scale(segment, flags_ref, images, images)
    grad_ref[...] = (mlp_scale * cot_ref[...].astype(F32)).astype(BF16)


def middle_forward(place, flags, mixed, x, cot, seg_column, bias, gain, shift, pieces, rows, tile=256):
    tokens, features = x.shape
    images = flags.shape[0] // 2
    row_block = pl.BlockSpec((tile, features), lambda t: (t, 0))
    half_block = pl.BlockSpec((tile, features // 2), lambda t: (t, 0))
    return pl.pallas_call(
        functools.partial(middle_kernel, rows, images),
        grid=(tokens // tile,),
        in_specs=[SMEM, SMEM, half_block, half_block, row_block, row_block, pl.BlockSpec((tile, 1), lambda t: (t, 0))]
        + [whole((1, features))] * 3
        + [ANY] * VIRTUAL,
        out_specs=[
            row_block,
            row_block,
            pl.BlockSpec((features, tile), lambda t: (0, t)),
            row_block,
            whole((features, features)),
        ],
        out_shape=[
            jax.ShapeDtypeStruct((tokens, features), F32),
            jax.ShapeDtypeStruct((tokens, features), BF16),
            jax.ShapeDtypeStruct((features, tokens), BF16),
            jax.ShapeDtypeStruct((tokens, features), BF16),
            jax.ShapeDtypeStruct((features, features), BF16),
        ],
        scratch_shapes=[pltpu.SemaphoreType.DMA((VIRTUAL,))],
        compiler_params=pltpu.CompilerParams(vmem_limit_bytes=48 << 20),
        cost_estimate=pl.CostEstimate(
            flops=2 * tokens * features * features, bytes_accessed=16 << 20, transcendentals=0
        ),
        name="middle_forward",
    )(place, flags, *mixed, x, cot, seg_column, bias, gain, shift, *pieces)


def split_shards(rows, place, source_ref, keep_ref, send_ref):
    for pair in range(VIRTUAL // 2):
        slot = pair ^ (place >> 1)
        stay = pl.multiple_of((2 * pair + (place & 1)) * rows, 16)
        leave = pl.multiple_of((2 * pair + 1 - (place & 1)) * rows, 16)
        keep_ref[slot] = source_ref[pl.ds(stay, rows), :]
        send_ref[slot] = source_ref[pl.ds(leave, rows), :]


root_half = 0.7071067811865476
root_two_pi_inverse = 0.3989422804014327


def mlp_kernel(
    rows, tiles, block, images, place_ref, flags_ref, normed_ref, normed_t_ref, g_ref, middle_ref, seg_ref, bias_out_ref, bias_ref, *refs
):
    pieces = refs[:VIRTUAL]
    (out_ref, gn_ref, keep1_ref, send1_ref, keep2_ref, send2_ref, db_ref) = refs[VIRTUAL : VIRTUAL + 7]
    w1_s, w2_s, act_s, gp_s, dw_s, branch_s, sems = refs[VIRTUAL + 7 :]
    f = pl.program_id(0)
    place = place_ref[0]
    tokens, features = normed_ref.shape
    hidden = w1_s.shape[1]
    parts = hidden // features

    @pl.when(f == 0)
    def _():
        copies = []
        for k in range(VIRTUAL):
            start = pl.multiple_of((place ^ k) * rows, 16)
            copies.append(
                pltpu.make_async_copy(
                    pieces[k].at[:, pl.ds(features, hidden)], w1_s.at[pl.ds(start, rows)], sems.at[0, k]
                )
            )
            for part in range(parts):
                start = pl.multiple_of(((place ^ k) * parts + part) * rows, 16)
                copies.append(
                    pltpu.make_async_copy(
                        pieces[k].at[:, pl.ds(features + hidden + part * features, features)],
                        w2_s.at[pl.ds(start, rows)],
                        sems.at[1 + part, k],
                    )
                )
        for copy in copies:
            copy.start()
        for copy in copies:
            copy.wait()

    first = pl.multiple_of(f * block, block)
    w1 = w1_s[:, pl.ds(first, block)]
    w2 = w2_s[pl.ds(first, block), :]
    bias = bias_ref[...]
    step = tokens // tiles
    db = jnp.zeros((1, block), F32)
    for t in range(tiles):
        part = slice(t * step, (t + 1) * step)
        pre = dot_nn(normed_ref[part, :], w1) + bias
        cdf = 0.5 * (1.0 + lax.erf(pre * root_half))
        act = (pre * cdf).astype(BF16)
        slope = cdf + pre * (jnp.exp(-0.5 * pre * pre) * root_two_pi_inverse)
        gp = (dot_nt(g_ref[part, :], w2) * slope).astype(BF16)
        db += jnp.sum(gp.astype(F32), axis=0, keepdims=True)
        act_s[part, :] = act
        gp_s[part, :] = gp
        out = dot_nn(act, w2)
        gn = dot_nt(gp, w1)

        @pl.when(f == 0)
        def _():
            branch_s[part, :] = out
            gn_ref[part, :] = gn

        @pl.when(f > 0)
        def _():
            branch_s[part, :] += out
            gn_ref[part, :] += gn

    @pl.when(f == pl.num_programs(0) - 1)
    def _():
        scale = branch_scale(seg_ref[...], flags_ref, images, images)
        out_ref[...] = (middle_ref[...] + scale * (branch_s[...] + bias_out_ref[...])).astype(BF16)

    db_ref[...] = db
    dw_s[...] = dot_nn(normed_t_ref[...], gp_s[...]).astype(BF16)
    split_shards(rows, place, dw_s, keep1_ref, send1_ref)
    dw_s[...] = dot_tn(act_s[...], g_ref[...]).astype(BF16)
    slot = f ^ (place >> 1)
    for part in range(parts):
        stay = pl.multiple_of(((place & 1) * parts + part) * rows, 16)
        leave = pl.multiple_of(((1 - (place & 1)) * parts + part) * rows, 16)
        columns = slice(part * features, (part + 1) * features)
        keep2_ref[slot, :, columns] = dw_s[pl.ds(stay, rows), :]
        send2_ref[slot, :, columns] = dw_s[pl.ds(leave, rows), :]


def mlp(place, flags, normed, normed_t, grads, middle, seg_column, bias_out, bias, pieces, rows, tiles=4):
    tokens, features = normed.shape
    hidden = bias.shape[1]
    parts = hidden // features
    block = 2 * hidden // VIRTUAL
    assert block == features
    half = VIRTUAL // 2
    columns = pl.BlockSpec((half, rows, block), lambda f: (0, 0, f))
    shards = jax.ShapeDtypeStruct((half, rows, hidden), BF16)
    images = flags.shape[0] // 2
    return pl.pallas_call(
        functools.partial(mlp_kernel, rows, tiles, block, images),
        grid=(hidden // block,),
        in_specs=[
            SMEM,
            SMEM,
            once((tokens, features)),
            once((features, tokens)),
            once((tokens, features)),
            once((tokens, features)),
            once((tokens, 1)),
            whole((1, features)),
            pl.BlockSpec((1, block), lambda f: (0, f)),
        ]
        + [ANY] * VIRTUAL,
        out_specs=[
            whole((tokens, features)),
            whole((tokens, features)),
            columns,
            columns,
            whole((half, rows, hidden)),
            whole((half, rows, hidden)),
            pl.BlockSpec((1, block), lambda f: (0, f)),
        ],
        out_shape=[jax.ShapeDtypeStruct((tokens, features), BF16), jax.ShapeDtypeStruct((tokens, features), F32)]
        + [shards] * 4
        + [jax.ShapeDtypeStruct((1, hidden), F32)],
        scratch_shapes=[
            pltpu.VMEM((features, hidden), BF16),
            pltpu.VMEM((hidden, features), BF16),
            pltpu.VMEM((tokens, block), BF16),
            pltpu.VMEM((tokens, block), BF16),
            pltpu.VMEM((features, block), BF16),
            pltpu.VMEM((tokens, features), F32),
            pltpu.SemaphoreType.DMA((1 + parts, VIRTUAL)),
        ],
        compiler_params=pltpu.CompilerParams(vmem_limit_bytes=62 << 20),
        cost_estimate=pl.CostEstimate(
            flops=12 * tokens * features * hidden,
            bytes_accessed=30 << 20,
            transcendentals=2 * tokens * hidden,
        ),
        name="mlp",
    )(place, flags, normed, normed_t, grads, middle, seg_column, bias_out, bias, *pieces)


def output_backward_kernel(
    rows, images, steps, place_ref, flags_ref, middle_ref, gn_ref, cot_ref, mixed0_ref, mixed1_ref, seg_ref,
    gain_ref, weight_ref, gm_ref, gx_ref, keep_ref, send_ref, sums_ref, dw_sum, dw_s,
):
    step = pl.program_id(0)
    segment = seg_ref[...]
    attn_scale = branch_scale(segment, flags_ref, 0, images)
    mlp_scale = branch_scale(segment, flags_ref, images, images)
    middle = middle_ref[...]
    cot = cot_ref[...].astype(F32)
    grad_b = (mlp_scale * cot).astype(BF16)
    gn = gn_ref[...]
    normal, inverse = norm_parts(middle)
    grad_middle = cot + norm_backward(normal, inverse, gn, gain_ref[...])
    gm_ref[...] = grad_middle
    grad_a = (attn_scale * grad_middle).astype(BF16)
    gx_ref[...] = dot_nt(grad_a, weight_ref[...]).astype(BF16)
    half = mixed0_ref.shape[1]
    accumulate(step, dw_sum.at[:half], dot_tn(mixed0_ref[...], grad_a))
    accumulate(step, dw_sum.at[half:], dot_tn(mixed1_ref[...], grad_a))
    total = lambda v: jnp.sum(v, axis=0, keepdims=True)
    sums = [total(gn * normal), total(gn), total(grad_a.astype(F32)), total(grad_b.astype(F32))]
    accumulate(step, sums_ref, jnp.concatenate(sums + [jnp.zeros((4,) + sums[0].shape[1:], F32)], axis=0))

    @pl.when(step == steps - 1)
    def _():
        dw_s[...] = dw_sum[...].astype(BF16)
        split_shards(rows, place_ref[0], dw_s, keep_ref, send_ref)


def output_backward(place, flags, middle, gn, cot, mixed, seg_column, gain, weight, rows, tile=256):
    tokens, features = middle.shape
    images = flags.shape[0] // 2
    half = VIRTUAL // 2
    steps = tokens // tile
    row_block = pl.BlockSpec((tile, features), lambda t: (t, 0))
    half_block = pl.BlockSpec((tile, features // 2), lambda t: (t, 0))
    shards = jax.ShapeDtypeStruct((half, rows, features), BF16)
    return pl.pallas_call(
        functools.partial(output_backward_kernel, rows, images, steps),
        grid=(steps,),
        in_specs=[SMEM, SMEM]
        + [row_block] * 3
        + [half_block] * 2
        + [pl.BlockSpec((tile, 1), lambda t: (t, 0)), whole((1, features)), whole((features, features))],
        out_specs=[row_block, row_block, whole((half, rows, features)), whole((half, rows, features)), whole((8, features))],
        out_shape=[
            jax.ShapeDtypeStruct((tokens, features), F32),
            jax.ShapeDtypeStruct((tokens, features), BF16),
            shards,
            shards,
            jax.ShapeDtypeStruct((8, features), F32),
        ],
        scratch_shapes=[pltpu.VMEM((features, features), F32), pltpu.VMEM((features, features), BF16)],
        compiler_params=pltpu.CompilerParams(vmem_limit_bytes=56 << 20),
        cost_estimate=pl.CostEstimate(
            flops=4 * tokens * features * features, bytes_accessed=22 << 20, transcendentals=0
        ),
        name="output_backward",
    )(place, flags, middle, gn, cot, *mixed, seg_column, gain, weight)


def joint_weight_kernel(rows, place_ref, normed_t_ref, dq_ref, dk_ref, dv_ref, keep_ref, send_ref, sums_ref, dw_s):
    step = pl.program_id(0)

    def block(ref):
        grads = ref[...]
        dw_s[...] = dot_nn(normed_t_ref[...], grads).astype(BF16)
        sums_ref[...] = jnp.sum(grads.astype(F32), axis=0, keepdims=True)

    for index, ref in enumerate((dq_ref, dk_ref, dv_ref)):
        pl.when(step == index)(functools.partial(block, ref))
    split_shards(rows, place_ref[0], dw_s, keep_ref, send_ref)


def joint_weight_grad(place, normed_t, dq, dk, dv, rows):
    features, tokens = normed_t.shape
    width = dq.shape[1]
    half = VIRTUAL // 2
    columns = pl.BlockSpec((half, rows, width), lambda c: (0, 0, c))
    shards = jax.ShapeDtypeStruct((half, rows, 3 * width), BF16)
    return pl.pallas_call(
        functools.partial(joint_weight_kernel, rows),
        grid=(3,),
        in_specs=[SMEM, whole((features, tokens))] + [whole((tokens, width))] * 3,
        out_specs=[columns, columns, pl.BlockSpec((1, width), lambda c: (0, c))],
        out_shape=[shards, shards, jax.ShapeDtypeStruct((1, 3 * width), F32)],
        scratch_shapes=[pltpu.VMEM((features, width), BF16)],
        compiler_params=pltpu.CompilerParams(vmem_limit_bytes=48 << 20),
        cost_estimate=pl.CostEstimate(
            flops=6 * tokens * features * width, bytes_accessed=6 << 20, transcendentals=0
        ),
        name="joint_weight_grad",
    )(place, normed_t, dq, dk, dv)


def joint_backward_kernel(*refs):
    grads = refs[:6]
    weight_ref, x_ref, gm_ref, gain_ref, gt_ref, sums_ref = refs[6:]
    features = x_ref.shape[1]
    width = features // 2
    gn = jnp.zeros(x_ref.shape, F32)
    for part in range(2):
        for index in range(3):
            start = index * features + part * width
            gn += dot_nt(grads[3 * part + index][...], weight_ref[:, start : start + width])
    normal, inverse = norm_parts(x_ref[...].astype(F32))
    gt_ref[...] = (gm_ref[...] + norm_backward(normal, inverse, gn, gain_ref[...])).astype(BF16)
    total = lambda v: jnp.sum(v, axis=0, keepdims=True)
    sums = [total(gn * normal), total(gn)]
    accumulate(
        pl.program_id(0), sums_ref, jnp.concatenate(sums + [jnp.zeros((6, features), F32)], axis=0)
    )


def joint_backward(grads, weight, x, gm, gain, tile=256):
    tokens, features = x.shape
    row_block = pl.BlockSpec((tile, features), lambda t: (t, 0))
    half_block = pl.BlockSpec((tile, features // 2), lambda t: (t, 0))
    return pl.pallas_call(
        joint_backward_kernel,
        grid=(tokens // tile,),
        in_specs=[half_block] * 6 + [whole((features, 3 * features)), row_block, row_block, whole((1, features))],
        out_specs=[row_block, whole((8, features))],
        out_shape=[jax.ShapeDtypeStruct((tokens, features), BF16), jax.ShapeDtypeStruct((8, features), F32)],
        compiler_params=pltpu.CompilerParams(vmem_limit_bytes=48 << 20),
        cost_estimate=pl.CostEstimate(
            flops=6 * tokens * features * features, bytes_accessed=15 << 20, transcendentals=0
        ),
        name="joint_backward",
    )(*grads, weight, x, gm, gain)


def after(value, *others):
    return lax.optimization_barrier((value, others))[0]


def dp_swap(value, bit):
    return lax.ppermute(value, "dp", [(i, i ^ bit) for i in range(VIRTUAL)])


def pick(value, place, parts):
    return lax.dynamic_index_in_dim(value, place % parts, 0, keepdims=False)


def seq_send(value, parts):
    me = lax.axis_index("seq")
    order = sorted(range(1, parts), key=lambda k: abs(k - parts / 2))
    return [
        (k, lax.ppermute(pick(value, me + k, parts), "seq", [(i, (i + k) % parts) for i in range(parts)]))
        for k in order
    ]


def seq_exchange(value, parts):
    return seq_place(value, seq_send(value, parts), parts)


def seq_place(value, got, parts):
    me = lax.axis_index("seq")
    out = lax.dynamic_update_index_in_dim(jnp.zeros_like(value), pick(value, me, parts), me, 0)
    for k, arrived in got:
        out = lax.dynamic_update_index_in_dim(out, arrived, (me - k) % parts, 0)
    return out


def interleave(mine, other):
    return [piece for both in zip(mine, other) for piece in both]


def add(left, right):
    return left.astype(F32) + right.astype(F32)


def seq_move(value, moves):
    return lax.ppermute(value, "seq", moves)


def chain_sum(value):
    value = value.astype(BF16)
    inner = add(value, seq_move(value, [(0, 1), (3, 2)])).astype(BF16)
    total = add(inner, seq_move(inner, [(1, 2), (2, 1)])).astype(BF16)
    back = seq_move(total, [(1, 0), (2, 3)])
    me = lax.axis_index("seq")
    return jnp.where((me == 1) | (me == 2), total, back).astype(F32)


def sum_everywhere(value, parts):
    for bit in (1, 2, 4):
        value = value + dp_swap(value, bit)
    if parts & (parts - 1):
        return lax.psum(value, "seq")
    bit = 1
    while bit < parts:
        value = value + lax.ppermute(value, "seq", [(i, i ^ bit) for i in range(parts)])
        bit *= 2
    return value


def pack_rows(matrix, rows):
    groups = matrix.shape[0] // rows
    return jnp.concatenate([matrix[g * rows : (g + 1) * rows] for g in range(groups)], axis=1)


def unpack_rows(matrix, features):
    groups = matrix.shape[1] // features
    return jnp.concatenate([matrix[:, g * features : (g + 1) * features] for g in range(groups)], axis=0)


def shards(
    ndp,
    nseq,
    tokens,
    cotangent,
    segments,
    keep_flags,
    first_gain,
    first_shift,
    joint_weight,
    joint_bias,
    output_weight,
    output_bias,
    second_gain,
    second_shift,
    expand_weight,
    expand_bias,
    reduce_weight,
    reduce_bias,
):
    row_count, shard_len, features = tokens.shape
    assert row_count == nseq
    row_len = segments.shape[1]
    hidden = expand_weight.shape[1]
    rows = features // VIRTUAL
    me_seq = lax.axis_index("seq")
    me_dp = lax.axis_index("dp")
    exact = ndp == VIRTUAL and nseq == 4

    smalls = (first_gain, first_shift, joint_bias, output_bias, second_gain, second_shift, expand_bias, reduce_bias)
    widths = [s.shape[0] * ndp for s in smalls]

    x = seq_exchange(tokens, nseq).reshape(row_len, features)

    if exact:
        place = me_dp.astype(jnp.int32).reshape(1)
        row = jnp.concatenate([s.astype(BF16) for s in smalls])
        width = 3 * features
        row = jnp.pad(row, (0, width - row.shape[0])).reshape(1, width)
        piece = jnp.concatenate([joint_weight.astype(BF16), jnp.pad(row, ((0, 15), (0, 0)))], axis=0)
        near = (dp_swap(piece, 2), dp_swap(piece, 4))
        own = [piece, near[0], near[1], dp_swap(near[0], 4)]
        joint_pieces = interleave(own, [dp_swap(p, 1) for p in own])
        small_slots = jnp.stack([p[rows, : sum(w // ndp for w in widths)] for p in joint_pieces]).astype(F32)
        slot = lax.broadcasted_iota(jnp.int32, (VIRTUAL, VIRTUAL, 1), 1)
        home = lax.broadcasted_iota(jnp.int32, (VIRTUAL, VIRTUAL, 1), 0)
        ordered = jnp.sum(jnp.where(slot == (home ^ me_dp), small_slots[None], 0.0), axis=1)
        params, start = [], 0
        for w in widths:
            params.append(ordered[:, start : start + w // ndp].reshape(1, w))
            start += w // ndp
        piece = jnp.concatenate(
            [output_weight.astype(BF16), expand_weight.astype(BF16), pack_rows(reduce_weight.astype(BF16), rows)],
            axis=1,
        )
        piece = after(piece, joint_pieces)
        own = [piece, dp_swap(piece, 2), dp_swap(piece, 4), dp_swap(piece, 6)]
        rest_pieces = interleave(own, [dp_swap(p, 1) for p in own])
    else:
        place = jnp.zeros((1,), jnp.int32)
        full = lambda w: lax.all_gather(w.astype(BF16), "dp", axis=0, tiled=True)
        params = [full(s).astype(F32).reshape(1, -1) for s in smalls]
        joint = full(joint_weight)
        out_w, up_w, down_w = full(output_weight), full(expand_weight), full(reduce_weight)
        joint_pieces = [joint[k * rows : (k + 1) * rows] for k in range(VIRTUAL)]
        group = hidden // VIRTUAL
        rest_pieces = [
            jnp.concatenate(
                [
                    out_w[k * rows : (k + 1) * rows],
                    up_w[k * rows : (k + 1) * rows],
                    pack_rows(down_w[k * group : (k + 1) * group], rows),
                ],
                axis=1,
            )
            for k in range(VIRTUAL)
        ]
    gain_a, shift_a, bias_qv, bias_out, gain_b, shift_b, bias_up, bias_down = params
    bias_joint = jnp.concatenate([bias_qv[:, :features], jnp.zeros((1, features), F32), bias_qv[:, features:]], axis=1)

    seg = lax.dynamic_index_in_dim(segments, me_seq, 0, keepdims=False)
    flags = lax.dynamic_index_in_dim(keep_flags, me_seq, 0, keepdims=False)
    seg_row, seg_column = seg.reshape(1, row_len), seg.reshape(row_len, 1)

    cot = seq_exchange(after(cotangent, x), nseq).reshape(row_len, features)

    proj, normed_a_t, weight_joint = joint_forward(place, x, gain_a, shift_a, bias_joint, joint_pieces, rows)
    first, totals_a = attention_forward(proj, seg_row, seg_column, 0, 2)
    if exact:
        proj_b = after(proj, first, own[1], own[2])
    else:
        proj_b = proj
    second, totals_b = attention_forward(proj_b, seg_row, seg_column, 1, 2)
    mixed = (first, second)
    middle, normed_b, normed_b_t, grad_b, weight_out = middle_forward(
        place, flags, mixed, x, cot, seg_column, bias_out, gain_b, shift_b, rest_pieces, rows
    )
    output, gn, keep_up, send_up, keep_down, send_down, g_bias_up = mlp(
        place, flags, normed_b, normed_b_t, grad_b, middle, seg_column, bias_down, bias_up, rest_pieces, rows
    )
    blocks_out = output.reshape(nseq, shard_len, features)
    sent_out = seq_send(blocks_out, nseq)
    if exact:
        moved_up, moved_down = dp_swap(send_up, 1), dp_swap(send_down, 1)
    grad_middle, grad_mixed, keep_out, send_out, sums_b = output_backward(
        place, flags, middle, gn, cot, mixed, seg_column, gain_b, weight_out, rows
    )
    early = jnp.concatenate([sums_b[2], sums_b[0], sums_b[1], g_bias_up[0], sums_b[3]])
    if exact:
        half_up = add(keep_up, moved_up).astype(BF16)
        half_down = add(keep_down, moved_down).astype(BF16)
        grad_mixed = after(grad_mixed, half_up, half_down)
        far_up, far_down = dp_swap(half_up[1::2], 2), dp_swap(half_down[2:], 4)
    grads_a = attention_backward(proj, grad_mixed, seg_row, seg_column, totals_a, 0, 2)
    keep_a, send_a, sums_joint_a = joint_weight_grad(place, normed_a_t, *grads_a, rows)
    if exact:
        one_up = add(half_up[0::2], far_up).astype(BF16)
        one_down = add(half_down[:2], far_down).astype(BF16)
        grad_mixed = after(grad_mixed, keep_a, one_up, one_down, sent_out)
        far_up, far_down = dp_swap(one_up[1], 4), dp_swap(one_down[1], 2)
        send_a = jnp.concatenate([send_a, send_out], axis=2)
        moved_a = dp_swap(send_a, 1)
    grads_b = attention_backward(proj, grad_mixed, seg_row, seg_column, totals_b, 1, 2)
    keep_b, send_b, sums_joint_b = joint_weight_grad(place, normed_a_t, *grads_b, rows)
    grads = grads_a + grads_b
    if exact:
        up = add(one_up[0], far_up)
        down = add(one_down[0], far_down)
        half_a = add(jnp.concatenate([keep_a, keep_out], axis=2), moved_a).astype(BF16)
        send_b = after(send_b, up, down, half_a)
        moved_b = dp_swap(send_b, 1)
        far_a = dp_swap(half_a[1::2], 2)
    grad_in, sums_a = joint_backward(grads, weight_joint, x, grad_middle, gain_a)

    output = seq_place(blocks_out, sent_out, nseq)
    grad_tokens = seq_exchange(grad_in.reshape(nseq, shard_len, features), nseq).astype(F32)

    width = features // 2
    sums_joint = [s[0, index * width : (index + 1) * width] for index in (0, 2) for s in (sums_joint_a, sums_joint_b)]
    late = jnp.concatenate([sums_a[0], sums_a[1]] + sums_joint)
    if exact:
        early = sum_everywhere(early.reshape(-1, 128), nseq).reshape(-1)
        late = sum_everywhere(late.reshape(-1, 128), nseq).reshape(-1)
        first = chain_sum(jnp.concatenate([up, down], axis=1))
        g_up = first[:, :hidden]
        g_down = unpack_rows(first[:, hidden:], features)
        half_b = add(keep_b, moved_b).astype(BF16)
        one_a = add(half_a[0::2], far_a).astype(BF16)
        part_a = add(one_a[0], dp_swap(one_a[1], 4))
        one_b = add(half_b[:2], dp_swap(half_b[2:], 4)).astype(BF16)
        part_b = add(one_b[0], dp_swap(one_b[1], 2))
        last = chain_sum(jnp.concatenate([part_a, part_b], axis=1))
        g_out = last[:, 3 * width : 3 * width + features]
        blocks = [last[:, c * width : (c + 1) * width] for c in (0, 5, 1, 6, 2, 7)]
        g_joint = jnp.concatenate(blocks, axis=1)
    else:
        early, late = lax.psum((early, late), ("dp", "seq"))

        def total(keep, send):
            return jnp.stack([keep, send], axis=1).reshape(features, keep.shape[2])

        def reduce(matrix):
            part = lax.psum_scatter(matrix.astype(F32), "dp", scatter_dimension=0, tiled=True)
            return lax.psum(part, "seq")

        g_up = reduce(total(keep_up, send_up))
        g_out = reduce(total(keep_out, send_out))
        joint_a, joint_b = total(keep_a, send_a), total(keep_b, send_b)
        blocks = [j[:, c * width : (c + 1) * width] for c in range(3) for j in (joint_a, joint_b)]
        g_joint = reduce(jnp.concatenate(blocks, axis=1))
        down = jnp.stack([keep_down, send_down], axis=1).reshape(VIRTUAL, rows, hidden)
        g_down = reduce(jnp.concatenate([unpack_rows(down[k], features) for k in range(VIRTUAL)], axis=0))

    def mine(vector, start, size):
        piece = size // ndp
        return lax.dynamic_slice_in_dim(vector, start + me_dp * piece, piece, 0)

    g_first_gain = mine(late, 0, features)
    g_first_shift = mine(late, features, features)
    g_joint_bias = mine(late, 2 * features, 2 * features)
    g_output_bias = mine(early, 0, features)
    g_second_gain = mine(early, features, features)
    g_second_shift = mine(early, 2 * features, features)
    g_expand_bias = mine(early, 3 * features, hidden)
    g_reduce_bias = mine(early, 3 * features + hidden, features)
    return (
        output,
        grad_tokens,
        g_first_gain,
        g_first_shift,
        g_joint,
        g_joint_bias,
        g_out,
        g_output_bias,
        g_second_gain,
        g_second_shift,
        g_up,
        g_expand_bias,
        g_down,
        g_reduce_bias,
    )


def solution(mesh):
    vector, matrix = P("dp"), P("dp", None)
    token_spec = P("dp", "seq", None)
    params = (vector, vector, matrix, vector, matrix, vector, vector, vector, matrix, vector, matrix, vector)
    return jax.shard_map(
        functools.partial(shards, mesh.shape["dp"], mesh.shape["seq"]),
        mesh=mesh,
        in_specs=(token_spec, token_spec, matrix, matrix) + params,
        out_specs=(token_spec, token_spec) + params,
        check_vma=False,
    )
```
